32 devices in a mesh: groups: 1, row: 32 (over z, y, x, core).
Axes of the slice: x: 2, y: 2, z: 4, core: 2. Of those that a mesh axis runs over, the one named last changes fastest.
Arguments:
- pair_mantissa: bfloat16 [128, 128, 128], P(('groups', 'row')), may hold values from -6 to 6
- pair_exponent: int32 [128, 1, 128], P(('groups', 'row')), may hold values from -3 to 3
- residue_mask: int32 [128], P('groups'), may hold values 0 or 1
- ln_gain: float32 [128], replicated, may hold values from 0.25 to 1.75
- ln_shift: float32 [128], replicated, may hold values from -3 to 3
- w_proj: bfloat16 [128, 512], replicated, may hold values from -10 to 10
- w_bias: bfloat16 [128, 4], replicated, may hold values from -0.5 to 0.5
- gate_shift: float32 [128], replicated, may hold values from -4 to 4
- w_out: bfloat16 [128, 128], replicated, may hold values from -0.5 to 0.5
- out_shift: float32 [128], replicated, may hold values from -3 to 3
Outputs:
- update: bfloat16 [32, 128, 128], P(('groups', 'row'))
The draws below stay inside these ranges and needn't reach their ends.
All inputs are finite; a program needn't handle non-finite values.
Results may differ from the reference program's by a relative error of at most 0.005.
Values may be sent and summed in bfloat16 or wider, within the bound.
A program may use at most 64 MiB of HBM per device.

```python
import jax
import jax.numpy as jnp
from jax import lax

C = 128
HEADS = 4
RD = 4
WD = 1
HD = 128
L = 128
SB = 128
N_ROW = 32


def shared_layer(key):
    base = jax.random.fold_in(key, 4093)
    keys = jax.random.split(base, 3)
    weights = jnp.clip(jax.random.normal(keys[2], (C, 4 * HD), jnp.float32), -6.0, 6.0) * C ** (-0.5)
    gain = 1.0 + 0.15 * jnp.clip(jax.random.normal(keys[0], (C,), jnp.float32), -5.0, 5.0)
    shift = 0.5 * jnp.clip(jax.random.normal(keys[1], (C,), jnp.float32), -6.0, 6.0)
    return (gain.astype(jnp.float32), shift.astype(jnp.float32), weights.astype(jnp.bfloat16))


def draw_ln_gain(key, part):
    return shared_layer(key)[0]


def draw_ln_shift(key, part):
    return shared_layer(key)[1]


def draw_w_proj(key, part):
    return shared_layer(key)[2]


def with_ends(values, own_key, smallest, top_value):
    place = [jax.random.randint(jax.random.fold_in(own_key, axis), (), 0, length) for axis, length in enumerate(values.shape)]
    widest = values.shape.index(max(values.shape))
    neighbour = place[:widest] + [(place[widest] + 1) % values.shape[widest]] + place[widest + 1:]
    return values.at[tuple(place)].set(smallest).at[tuple(neighbour)].set(top_value)


def levels(rng, dims, cuts, low, high):
    level, own = 1.0, jax.random.fold_in(rng, 6)
    for position, parts in cuts:
        draws = jnp.exp(jax.random.uniform(jax.random.fold_in(own, position), (parts,), jnp.float32, low / len(cuts), high / len(cuts)))
        level = level * jnp.repeat(draws, dims[position] // parts).reshape([-1 if axis == position else 1 for axis in range(len(dims))])
    return level


def centred(own_key, dims, width, most, pieces=(), kind=jnp.bfloat16):
    values = width * jax.random.normal(own_key, dims, jnp.float32)
    if pieces:
        values = values * levels(own_key, dims, pieces, -0.22, 0.18)
    return jnp.clip(values, -most, most).astype(kind)


def setup_inputs(seed: int = 0, part: int = 0) -> dict:
    key_list = jax.random.split(jax.random.key(seed), 11)
    part_keys = jax.random.split(jax.random.fold_in(key_list[10], part), 11)
    return {
        "pair_mantissa": centred(part_keys[0], (L, L, C), 1.0, 6.0, ((0, 32),)),
        "pair_exponent": with_ends(jax.random.randint(part_keys[1], (L, L // SB, C), -3, 4), jax.random.fold_in(part_keys[1], 1), -3, 3).astype(jnp.int32),
        "residue_mask": with_ends((jax.random.randint(part_keys[2], (L,), 0, 8) < 7).astype(jnp.int32), jax.random.fold_in(part_keys[2], 1), 0, 1),
        "ln_gain": draw_ln_gain(jax.random.fold_in(key_list[10], 71), part),
        "ln_shift": draw_ln_shift(jax.random.fold_in(key_list[10], 71), part),
        "w_proj": draw_w_proj(jax.random.fold_in(key_list[10], 71), part),
        "w_bias": centred(key_list[6], (C, HEADS), C ** -0.5, 0.5),
        "gate_shift": centred(key_list[7], (HD,), 1.0, 4.0, (), jnp.float32),
        "w_out": centred(key_list[8], (HD, C), HD ** -0.5, 0.5),
        "out_shift": centred(key_list[9], (C,), 0.5, 3.0, (), jnp.float32),
    }


epsilon = 1e-05
big_negative = 1000000000.0

def dequantize(mantissa, exponent):
    scaling = jnp.zeros(exponent.shape, jnp.float32)
    for expo_level in range(-3, 4):
        scaling = scaling + jnp.where(exponent == expo_level, jnp.float32(2.0 ** expo_level), jnp.float32(0.0))
    row_count, block_count, channels = exponent.shape
    block_width = mantissa.shape[1] // block_count
    scaling = jnp.broadcast_to(scaling[:, :, None, :], (row_count, block_count, block_width, channels))
    return mantissa.astype(jnp.float32) * scaling.reshape(row_count, block_count * block_width, channels)

def normalize(mantissa, exponent, ln_gain, ln_shift):
    values = dequantize(mantissa, exponent)
    center = lax.optimization_barrier(jnp.mean(values, axis=-1, keepdims=True))
    spread = lax.optimization_barrier(jnp.mean(jnp.square(values - center), axis=-1, keepdims=True))
    return ((values - center) * lax.rsqrt(spread + epsilon) * ln_gain + ln_shift).astype(jnp.bfloat16)

def column_block(columns, key_bias, mask_bias, w_proj, gate_shift, w_out, out_shift):
    inner_width = w_out.shape[0]
    head_count = key_bias.shape[1]
    head_size = inner_width // head_count
    window_rows = key_bias.shape[2]
    as_float = columns.astype(jnp.float32)
    high = lax.Precision.HIGHEST
    key_value = jnp.einsum('lmc,cd->mld', as_float, w_proj[:, inner_width:3 * inner_width].astype(jnp.float32), precision=high).astype(jnp.bfloat16)
    query_weight = jnp.concatenate([w_proj[:, :inner_width], w_proj[:, 3 * inner_width:]], axis=1).astype(jnp.float32)
    query_gate = jnp.einsum('wmc,cd->mwd', as_float[:window_rows], query_weight, precision=high)
    queries = (query_gate[..., :inner_width] * head_size ** (-0.5)).astype(jnp.bfloat16)
    gating = jax.nn.sigmoid(query_gate[..., inner_width:] + gate_shift)
    bias_float = key_bias.astype(jnp.float32)

    def single_column(operands):
        kv_column, query_column, gate_column = operands
        kv_float = lax.optimization_barrier(kv_column).astype(jnp.float32)
        key_heads = kv_float[:, :inner_width].reshape(-1, head_count, head_size)
        value_heads = kv_float[:, inner_width:].reshape(-1, head_count, head_size)
        query_heads = lax.optimization_barrier(query_column).astype(jnp.float32).reshape(window_rows, head_count, head_size)
        scores = jnp.einsum('lhd,whd->lhw', key_heads, query_heads, precision=high) + bias_float + mask_bias[:, None, None]
        row_max = lax.optimization_barrier(jnp.max(scores, axis=0))
        weights = jnp.exp(scores - row_max)
        denominator = lax.optimization_barrier(jnp.sum(weights, axis=0))
        rounded = lax.optimization_barrier(weights.astype(jnp.bfloat16)).astype(jnp.float32)
        attended = jnp.einsum('lhw,lhd->whd', rounded, value_heads, precision=high)
        attended = attended / denominator.T[:, :, None]
        gated_out = (gate_column * attended.reshape(window_rows, inner_width)).astype(jnp.bfloat16)
        return (jnp.dot(gated_out, w_out, preferred_element_type=jnp.float32) + out_shift).astype(jnp.bfloat16)
    return lax.map(single_column, (key_value, queries, gating))

def reference(pair_mantissa, pair_exponent, residue_mask, ln_gain, ln_shift, w_proj, w_bias, gate_shift, w_out, out_shift):
    length = pair_mantissa.shape[0]
    channels = pair_mantissa.shape[2]
    window_rows = WD * N_ROW
    block_count = length // RD
    exponent_blocks = pair_exponent.shape[1]
    share = length // exponent_blocks
    mantissa_rows = pair_mantissa.reshape(block_count, RD, length, channels)
    exponent_rows = pair_exponent.reshape(block_count, RD, exponent_blocks, channels)

    def bias_block(operands):
        normal_rows = normalize(operands[0], operands[1], ln_gain, ln_shift)
        return jnp.einsum('rwc,ch->rhw', normal_rows[:, :window_rows].astype(jnp.float32), w_bias.astype(jnp.float32), precision=lax.Precision.HIGHEST).astype(jnp.bfloat16)
    key_bias = lax.map(bias_block, (mantissa_rows, exponent_rows)).reshape(length, w_bias.shape[1], window_rows)
    mask_bias = big_negative * (residue_mask.astype(jnp.float32) - 1.0)

    def one_block(block):
        start = (block * RD).astype(jnp.int32)
        columns = lax.dynamic_slice_in_dim(pair_mantissa, start, RD, 1)
        exponent_column = lax.dynamic_slice_in_dim(pair_exponent, (start // share).astype(jnp.int32), 1, 1)
        normal_columns = normalize(columns, exponent_column, ln_gain, ln_shift)
        return column_block(normal_columns, key_bias, mask_bias, w_proj, gate_shift, w_out, out_shift)
    result = lax.map(one_block, jnp.arange(block_count, dtype=jnp.int32)).reshape(length, window_rows, channels)
    return jnp.transpose(result, (1, 0, 2))
```

```python
import functools

import jax
import jax.numpy as jnp
from jax import lax
from jax.experimental import pallas as pl
from jax.experimental.pallas import tpu as pltpu
from jax.sharding import PartitionSpec as P

WD = 1

epsilon = 1e-05
big_negative = 1000000000.0
MESH = pl.DeviceIdType.MESH
F32 = jnp.float32
BF16 = jnp.bfloat16


def dot(a, b, ca=1, cb=0):
    return lax.dot_general(a, b, (((ca,), (cb,)), ((), ())), preferred_element_type=F32)


def head_mask(rows, lanes, row_group, lane_group):
    row_head = lax.broadcasted_iota(jnp.int32, (rows, lanes), 0) // row_group
    lane_head = lax.broadcasted_iota(jnp.int32, (rows, lanes), 1) // lane_group
    return row_head == lane_head


def each_peer(n, body):
    if n <= 32:
        for step in range(1, n):
            body(step)
    else:
        lax.fori_loop(1, n, lambda step, _: (body(step), 0)[1], 0)


def kernel(
    n, heads,
    mant_hbm, expo_hbm, mask_hbm, gain_hbm, shift_hbm, proj_hbm, wbias_hbm, gate_hbm, wout_hbm, oshift_hbm,
    out_ref,
    mant, expo, mask, gain, shift, proj, wbias, gate, wout, oshift,
    send, recv, bias_send, bias_recv, rows, mixed, back,
    load_sems, send_sems, recv_sems,
):
    me = lax.axis_index("row")
    local, length, channels = mant.shape
    inner = wout.shape[0]
    window = WD * n
    size = inner // heads
    lanes = heads * window

    barrier = pltpu.get_barrier_semaphore()
    loads = [
        pltpu.make_async_copy(src, dst, load_sems.at[number])
        for number, (src, dst) in enumerate(
            [
                (mant_hbm, mant), (expo_hbm, expo), (gain_hbm, gain), (shift_hbm, shift), (wbias_hbm, wbias),
                (mask_hbm, mask), (proj_hbm, proj), (gate_hbm, gate), (wout_hbm, wout), (oshift_hbm, oshift),
            ]
        )
    ]
    for load in loads:
        load.start()

    def greet(step):
        pl.semaphore_signal(barrier, inc=1, device_id={"row": lax.rem(me + step, n)}, device_id_type=MESH)

    each_peer(n, greet)

    for load in loads[:5]:
        load.wait()
    exponent = expo[...]
    scaling = jnp.zeros(exponent.shape, F32)
    for level in range(-3, 4):
        scaling = scaling + jnp.where(exponent == level, F32(2.0**level), F32(0.0))
    blocks = exponent.shape[1]
    values = mant[...].astype(F32).reshape(local, blocks, length // blocks, channels) * scaling[:, :, None, :]
    values = values.reshape(local * length, channels)
    center = jnp.mean(values, axis=-1, keepdims=True)
    values = values - center
    spread = jnp.mean(jnp.square(values), axis=-1, keepdims=True)
    normal = values * lax.rsqrt(spread + epsilon) * gain[...] + shift[...]

    split = normal.reshape(local, length // 8, 8, channels)
    low = lax.broadcasted_iota(jnp.int32, (length // 8, 8, channels), 1) < local
    even, odd = [], []
    for pair in range(0, local, 2):
        one, two = split[pair], split[pair + 1]
        even.append(jnp.where(low, one, pltpu.roll(two, local, 1)))
        odd.append(jnp.where(low, pltpu.roll(one, local, 1), two))
    send[:, 0] = jnp.concatenate(even, axis=1).astype(BF16)
    send[:, 1] = jnp.concatenate(odd, axis=1).astype(BF16)

    rounded = normal.astype(BF16).reshape(local, length, channels)
    bias_mask = head_mask(heads, lanes, 1, window)
    local_bias = []
    for row in range(local):
        repeated = jnp.concatenate([rounded[row, :window]] * heads, axis=0)
        product = dot(wbias[...], repeated, 1, 1)
        local_bias.append(jnp.sum(jnp.where(bias_mask, product, 0.0), axis=0, keepdims=True))
    bias_send[...] = jnp.concatenate(local_bias, axis=0).astype(BF16)

    for load in loads[5:]:
        load.wait()
    mask_row = big_negative * (mask[...].astype(F32) - 1.0)
    mask_column = jnp.broadcast_to(mask_row, (128, length)).T[:, :1]

    pl.semaphore_wait(barrier, n - 1)

    def pair_of(peer):
        return peer // 2, lax.rem(peer, 2)

    def scatter(step):
        peer = lax.rem(me + step, n)
        high, parity = pair_of(peer)
        pltpu.make_async_remote_copy(
            src_ref=send.at[high, parity], dst_ref=recv.at[me],
            send_sem=send_sems.at[0], recv_sem=recv_sems.at[0],
            device_id={"row": peer}, device_id_type=MESH,
        ).start()

    def spread_bias(step):
        peer = lax.rem(me + step, n)
        pltpu.make_async_remote_copy(
            src_ref=bias_send, dst_ref=bias_recv.at[me],
            send_sem=send_sems.at[1], recv_sem=recv_sems.at[1],
            device_id={"row": peer}, device_id_type=MESH,
        ).start()

    each_peer(n, scatter)
    each_peer(n, spread_bias)
    high, parity = pair_of(me)
    recv[me] = send[high, parity]
    bias_recv[me] = bias_send[...]

    def wait_all(ref, semaphore):
        whole = ref.at[pl.ds(0, n - 1)]
        pltpu.make_async_copy(whole, whole, semaphore).wait()

    wait_all(recv, recv_sems.at[0])
    wait_all(bias_recv, recv_sems.at[1])

    rows[...] = recv[...].astype(F32).reshape(n * local * local, channels)
    keys_count = n * local
    columns = [rows[pl.ds(column, keys_count, stride=local), :].astype(BF16) for column in range(local)]
    bias = bias_recv[...].astype(F32).reshape(keys_count, lanes)
    query_mask = head_mask(lanes, inner, window, size)
    key_value = dot(jnp.concatenate(columns, axis=0), proj[:, inner : 3 * inner]).astype(BF16)
    tops = jnp.concatenate([column[:window] for column in columns], axis=0)
    queries = dot(tops, proj[:, :inner]) * size ** (-0.5)
    gating = jax.nn.sigmoid(dot(tops, proj[:, 3 * inner :]) + gate[...])
    attended = []
    for column in range(local):
        keys = key_value[column * keys_count : (column + 1) * keys_count, :inner]
        held = key_value[column * keys_count : (column + 1) * keys_count, inner:]
        query = queries[column * window : (column + 1) * window]
        query = jnp.where(query_mask, jnp.concatenate([query] * heads, axis=0), 0.0).astype(BF16)
        scores = dot(keys, query, 1, 1) + bias + mask_column
        weights = jnp.exp(scores - jnp.max(scores, axis=0, keepdims=True))
        totals = jnp.sum(weights, axis=0, keepdims=True)
        weights = (weights / totals).astype(BF16)
        mixture = jnp.where(query_mask, dot(weights, held, 0, 0), 0.0)
        attended.append(jnp.sum(mixture.reshape(heads, window, inner), axis=0))
    gated = (gating * jnp.concatenate(attended, axis=0)).astype(BF16)
    update = dot(gated, wout[...]) + oshift[...]
    for column in range(local):
        mixed[pl.ds(column, window, stride=local), :] = update[column * window : (column + 1) * window]
    back[...] = mixed[...].reshape(n, WD * local, channels).astype(BF16)

    def give_back(step):
        peer = lax.rem(me + step, n)
        pltpu.make_async_remote_copy(
            src_ref=back.at[peer], dst_ref=out_ref.at[me],
            send_sem=send_sems.at[2], recv_sem=recv_sems.at[2],
            device_id={"row": peer}, device_id_type=MESH,
        ).start()

    each_peer(n, give_back)
    out_ref[me] = back[me]
    wait_all(out_ref, recv_sems.at[2])
    wait_all(recv, send_sems.at[0])
    wait_all(bias_recv, send_sems.at[1])
    wait_all(out_ref, send_sems.at[2])


def per_device(
    pair_mantissa,
    pair_exponent,
    residue_mask,
    ln_gain,
    ln_shift,
    w_proj,
    w_bias,
    gate_shift,
    w_out,
    out_shift,
):
    n = lax.axis_size("row")
    local, length, channels = pair_mantissa.shape
    heads = w_bias.shape[1]
    lanes = heads * WD * n
    args = (
        pair_mantissa, pair_exponent, residue_mask[None], ln_gain[None], ln_shift[None],
        w_proj, w_bias.T, gate_shift[None], w_out, out_shift[None],
    )
    result = pl.pallas_call(
        functools.partial(kernel, n, heads),
        out_shape=jax.ShapeDtypeStruct((n, WD * local, channels), BF16),
        in_specs=[pl.BlockSpec(memory_space=pl.ANY)] * len(args),
        out_specs=pl.BlockSpec(memory_space=pltpu.VMEM),
        scratch_shapes=[pltpu.VMEM(arg.shape, arg.dtype) for arg in args]
        + [
            pltpu.VMEM((n // 2, 2, local * local, channels), BF16),
            pltpu.VMEM((n, local * local, channels), BF16),
            pltpu.VMEM((local, lanes), BF16),
            pltpu.VMEM((n, local, lanes), BF16),
            pltpu.VMEM((n * local * local, channels), F32),
            pltpu.VMEM((n * WD * local, channels), F32),
            pltpu.VMEM((n, WD * local, channels), BF16),
            pltpu.SemaphoreType.DMA((len(args),)),
            pltpu.SemaphoreType.DMA((3,)),
            pltpu.SemaphoreType.DMA((3,)),
        ],
        compiler_params=pltpu.CompilerParams(collective_id=0, has_side_effects=True),
    )(*args)
    return result.reshape(WD, length, channels)


def solution(mesh):
    in_specs = (
        P(("groups", "row"), None, None),
        P(("groups", "row"), None, None),
        P("groups"),
        P(),
        P(),
        P(),
        P(),
        P(),
        P(),
        P(),
    )
    out_specs = P(("groups", "row"), None, None)
    return jax.shard_map(
        per_device, mesh=mesh, in_specs=in_specs, out_specs=out_specs, check_vma=False
    )
```

```python
import functools

import jax
import jax.numpy as jnp
from jax import lax
from jax.experimental import pallas as pl
from jax.experimental.pallas import tpu as pltpu
from jax.sharding import PartitionSpec as P

WD = 1

epsilon = 1e-05
big_negative = 1000000000.0
LOGICAL = pl.DeviceIdType.LOGICAL
F32 = jnp.float32
BF16 = jnp.bfloat16


def dot(a, b, ca=1, cb=0):
    return lax.dot_general(a, b, (((ca,), (cb,)), ((), ())), preferred_element_type=F32)


def head_mask(rows, lanes, row_group, lane_group):
    row_head = lax.broadcasted_iota(jnp.int32, (rows, lanes), 0) // row_group
    lane_head = lax.broadcasted_iota(jnp.int32, (rows, lanes), 1) // lane_group
    return row_head == lane_head


def each_peer(n, body):
    for step in range(n - 1, 0, -1):
        body(step)


def kernel(
    n, heads,
    mant_hbm, expo_hbm, mask_hbm, gain_hbm, shift_hbm, proj_hbm, wbias_hbm, gate_hbm, wout_hbm, oshift_hbm,
    out_ref,
    mant, expo, mask, gain, shift, proj, wbias, gate, wout, oshift,
    send, recv, bias_send, bias_recv, rows, mixed, back,
    load_sems, send_sems, recv_sems,
):
    me = lax.axis_index("row")
    base = lax.axis_index("groups") * n

    flips, rest = [], me
    while len(flips) < (n - 1).bit_length():
        flips.append((1 - 2 * lax.rem(rest, 2)) * 2 ** len(flips))
        rest = rest // 2

    def peer_of(step):
        return me + sum(flip for bit, flip in enumerate(flips) if step >> bit & 1)

    local, length, channels = mant.shape
    inner = wout.shape[0]
    window = WD * n
    size = inner // heads
    lanes = heads * window

    barrier = pltpu.get_barrier_semaphore()

    def greet(step):
        pl.semaphore_signal(barrier, inc=1, device_id=base + peer_of(step), device_id_type=LOGICAL)

    each_peer(n, greet)

    loads = [
        pltpu.make_async_copy(src, dst, load_sems.at[number])
        for number, (src, dst) in enumerate(
            [
                (mant_hbm, mant), (expo_hbm, expo), (gain_hbm, gain), (shift_hbm, shift), (wbias_hbm, wbias),
                (mask_hbm, mask), (proj_hbm, proj), (gate_hbm, gate), (wout_hbm, wout), (oshift_hbm, oshift),
            ]
        )
    ]
    for load in loads:
        load.start()

    for load in loads[:5]:
        load.wait()
    exponent = expo[...]
    scaling = jnp.zeros(exponent.shape, F32)
    for level in range(-3, 4):
        scaling = scaling + jnp.where(exponent == level, F32(2.0**level), F32(0.0))
    blocks = exponent.shape[1]
    values = mant[...].astype(F32).reshape(local, blocks, length // blocks, channels) * scaling[:, :, None, :]
    values = values.reshape(local * length, channels)
    center = jnp.mean(values, axis=-1, keepdims=True)
    values = values - center
    spread = jnp.mean(jnp.square(values), axis=-1, keepdims=True)
    normal = values * lax.rsqrt(spread + epsilon) * gain[...] + shift[...]

    split = normal.reshape(local, length // 8, 8, channels)
    low = lax.broadcasted_iota(jnp.int32, (length // 8, 8, channels), 1) < local
    even, odd = [], []
    for pair in range(0, local, 2):
        one, two = split[pair], split[pair + 1]
        even.append(jnp.where(low, one, pltpu.roll(two, local, 1)))
        odd.append(jnp.where(low, pltpu.roll(one, local, 1), two))
    pairs = jnp.stack([jnp.concatenate(even, axis=1), jnp.concatenate(odd, axis=1)], axis=1)
    send[...] = pairs.reshape(n, local * local, channels).astype(BF16)

    rounded = normal.astype(BF16).reshape(local, length, channels)
    bias_mask = head_mask(heads, lanes, 1, window)
    local_bias = []
    for row in range(local):
        repeated = jnp.concatenate([rounded[row, :window]] * heads, axis=0)
        product = dot(wbias[...], repeated, 1, 1)
        local_bias.append(jnp.sum(jnp.where(bias_mask, product, 0.0), axis=0, keepdims=True))
    bias_send[...] = jnp.concatenate(local_bias, axis=0).astype(BF16)

    for load in loads[5:]:
        load.wait()
    mask_row = big_negative * (mask[...].astype(F32) - 1.0)
    mask_column = jnp.broadcast_to(mask_row, (128, length)).T[:, :1]

    pl.semaphore_wait(barrier, n - 1)

    def scatter(step):
        peer = peer_of(step)
        pltpu.make_async_remote_copy(
            src_ref=send.at[peer], dst_ref=recv.at[me],
            send_sem=send_sems.at[0], recv_sem=recv_sems.at[0],
            device_id=base + peer, device_id_type=LOGICAL,
        ).start()

    def spread_bias(step):
        peer = peer_of(step)
        pltpu.make_async_remote_copy(
            src_ref=bias_send, dst_ref=bias_recv.at[me],
            send_sem=send_sems.at[1], recv_sem=recv_sems.at[1],
            device_id=base + peer, device_id_type=LOGICAL,
        ).start()

    each_peer(n, scatter)
    each_peer(n, spread_bias)
    recv[me] = send[me]
    bias_recv[me] = bias_send[...]

    def wait_all(ref, semaphore):
        whole = ref.at[pl.ds(0, n - 1)]
        pltpu.make_async_copy(whole, whole, semaphore).wait()

    wait_all(recv, recv_sems.at[0])

    rows[...] = recv[...].astype(F32).reshape(n * local * local, channels)
    keys_count = n * local
    columns = [rows[pl.ds(column, keys_count, stride=local), :].astype(BF16) for column in range(local)]
    query_mask = head_mask(lanes, inner, window, size)
    key_value = dot(jnp.concatenate(columns, axis=0), proj[:, inner : 3 * inner]).astype(BF16)
    tops = jnp.concatenate([column[:window] for column in columns], axis=0)
    queries = dot(tops, proj[:, :inner]) * size ** (-0.5)
    gating = jax.nn.sigmoid(dot(tops, proj[:, 3 * inner :]) + gate[...])
    wait_all(bias_recv, recv_sems.at[1])
    bias = bias_recv[...].astype(F32).reshape(keys_count, lanes)
    attended = []
    for column in range(local):
        keys = key_value[column * keys_count : (column + 1) * keys_count, :inner]
        held = key_value[column * keys_count : (column + 1) * keys_count, inner:]
        query = queries[column * window : (column + 1) * window]
        query = jnp.where(query_mask, jnp.concatenate([query] * heads, axis=0), 0.0).astype(BF16)
        scores = dot(keys, query, 1, 1) + bias + mask_column
        weights = jnp.exp(scores - jnp.max(scores, axis=0, keepdims=True))
        totals = jnp.sum(weights, axis=0, keepdims=True)
        weights = (weights / totals).astype(BF16)
        mixture = jnp.where(query_mask, dot(weights, held, 0, 0), 0.0)
        attended.append(jnp.sum(mixture.reshape(heads, window, inner), axis=0))
    gated = (gating * jnp.concatenate(attended, axis=0)).astype(BF16)
    update = dot(gated, wout[...]) + oshift[...]
    for column in range(local):
        mixed[pl.ds(column, window, stride=local), :] = update[column * window : (column + 1) * window]
    back[...] = mixed[...].reshape(n, WD * local, channels).astype(BF16)

    def give_back(step):
        peer = peer_of(step)
        pltpu.make_async_remote_copy(
            src_ref=back.at[peer], dst_ref=out_ref.at[me],
            send_sem=send_sems.at[2], recv_sem=recv_sems.at[2],
            device_id=base + peer, device_id_type=LOGICAL,
        ).start()

    each_peer(n, give_back)
    out_ref[me] = back[me]
    wait_all(out_ref, recv_sems.at[2])
    wait_all(recv, send_sems.at[0])
    wait_all(bias_recv, send_sems.at[1])
    wait_all(out_ref, send_sems.at[2])


def per_device(
    pair_mantissa,
    pair_exponent,
    residue_mask,
    ln_gain,
    ln_shift,
    w_proj,
    w_bias,
    gate_shift,
    w_out,
    out_shift,
):
    n = lax.axis_size("row")
    local, length, channels = pair_mantissa.shape
    heads = w_bias.shape[1]
    lanes = heads * WD * n
    args = (
        pair_mantissa, pair_exponent, residue_mask[None], ln_gain[None], ln_shift[None],
        w_proj, w_bias.T, gate_shift[None], w_out, out_shift[None],
    )
    result = pl.pallas_call(
        functools.partial(kernel, n, heads),
        out_shape=pltpu.VMEM((n, WD * local, channels), BF16),
        in_specs=[pl.BlockSpec(memory_space=pl.ANY)] * len(args),
        out_specs=pl.BlockSpec(memory_space=pltpu.VMEM),
        scratch_shapes=[pltpu.VMEM(arg.shape, arg.dtype) for arg in args]
        + [
            pltpu.VMEM((n, local * local, channels), BF16),
            pltpu.VMEM((n, local * local, channels), BF16),
            pltpu.VMEM((local, lanes), BF16),
            pltpu.VMEM((n, local, lanes), BF16),
            pltpu.VMEM((n * local * local, channels), F32),
            pltpu.VMEM((n * WD * local, channels), F32),
            pltpu.VMEM((n, WD * local, channels), BF16),
            pltpu.SemaphoreType.DMA((len(args),)),
            pltpu.SemaphoreType.DMA((3,)),
            pltpu.SemaphoreType.DMA((3,)),
        ],
        compiler_params=pltpu.CompilerParams(collective_id=0, has_side_effects=True),
    )(*args)
    return result.reshape(WD, length, channels)


def solution(mesh):
    in_specs = (
        P(("groups", "row"), None, None),
        P(("groups", "row"), None, None),
        P("groups"),
        P(),
        P(),
        P(),
        P(),
        P(),
        P(),
        P(),
    )
    out_specs = P(("groups", "row"), None, None)
    return jax.shard_map(
        per_device, mesh=mesh, in_specs=in_specs, out_specs=out_specs, check_vma=False
    )
```

```python
import functools

import jax
import jax.numpy as jnp
from jax import lax
from jax.experimental import pallas as pl
from jax.experimental.pallas import tpu as pltpu
from jax.sharding import PartitionSpec as P

WD = 1

epsilon = 1e-05
big_negative = 1000000000.0
LOGICAL = pl.DeviceIdType.LOGICAL
F32 = jnp.float32
BF16 = jnp.bfloat16


def dot(a, b, ca=1, cb=0):
    return lax.dot_general(a, b, (((ca,), (cb,)), ((), ())), preferred_element_type=F32)


def head_mask(rows, lanes, row_group, lane_group):
    row_head = lax.broadcasted_iota(jnp.int32, (rows, lanes), 0) // row_group
    lane_head = lax.broadcasted_iota(jnp.int32, (rows, lanes), 1) // lane_group
    return row_head == lane_head


def each_peer(n, body):
    for step in range(n - 1, 0, -1):
        body(step)


def kernel(
    n, heads,
    mant_hbm, expo_hbm, mask_hbm, gain_hbm, shift_hbm, proj_hbm, wbias_hbm, gate_hbm, wout_hbm, oshift_hbm,
    out_ref,
    mant, expo, mask, gain, shift, proj, wbias, gate, wout, oshift,
    send, recv, bias_send, bias_recv, rows, mixed, back,
    load_sems, send_sems, recv_sems, swap_sems,
):
    me = lax.axis_index("row")
    base = lax.axis_index("groups") * n

    flips, rest = [], me
    while len(flips) < (n - 1).bit_length():
        flips.append((1 - 2 * lax.rem(rest, 2)) * 2 ** len(flips))
        rest = rest // 2

    def peer_of(step):
        return me + sum(flip for bit, flip in enumerate(flips) if step >> bit & 1)

    local, length, channels = mant.shape
    inner = wout.shape[0]
    window = WD * n
    size = inner // heads
    lanes = heads * window

    barrier = pltpu.get_barrier_semaphore()

    def greet(step):
        pl.semaphore_signal(barrier, inc=1, device_id=base + peer_of(step), device_id_type=LOGICAL)

    each_peer(n, greet)

    loads = [
        pltpu.make_async_copy(src, dst, load_sems.at[number])
        for number, (src, dst) in enumerate(
            [
                (mant_hbm, mant), (expo_hbm, expo), (gain_hbm, gain), (shift_hbm, shift), (wbias_hbm, wbias),
                (mask_hbm, mask), (proj_hbm, proj), (gate_hbm, gate), (wout_hbm, wout), (oshift_hbm, oshift),
            ]
        )
    ]
    for load in loads:
        load.start()

    for load in loads[:5]:
        load.wait()
    exponent = expo[...]
    scaling = jnp.zeros(exponent.shape, F32)
    for level in range(-3, 4):
        scaling = scaling + jnp.where(exponent == level, F32(2.0**level), F32(0.0))
    blocks = exponent.shape[1]
    values = mant[...].astype(F32).reshape(local, blocks, length // blocks, channels) * scaling[:, :, None, :]
    values = values.reshape(local * length, channels)
    center = jnp.mean(values, axis=-1, keepdims=True)
    values = values - center
    spread = jnp.mean(jnp.square(values), axis=-1, keepdims=True)
    normal = values * lax.rsqrt(spread + epsilon) * gain[...] + shift[...]

    split = normal.reshape(local, length // 8, 8, channels)
    low = lax.broadcasted_iota(jnp.int32, (length // 8, 8, channels), 1) < local
    even, odd = [], []
    for pair in range(0, local, 2):
        one, two = split[pair], split[pair + 1]
        even.append(jnp.where(low, one, pltpu.roll(two, local, 1)))
        odd.append(jnp.where(low, pltpu.roll(one, local, 1), two))
    pairs = jnp.stack([jnp.concatenate(even, axis=1), jnp.concatenate(odd, axis=1)], axis=1)
    send[...] = pairs.reshape(n, local * local, channels).astype(BF16)

    rounded = normal.astype(BF16).reshape(local, length, channels)
    bias_mask = head_mask(heads, lanes, 1, window)
    local_bias = []
    for row in range(local):
        repeated = jnp.concatenate([rounded[row, :window]] * heads, axis=0)
        product = dot(wbias[...], repeated, 1, 1)
        local_bias.append(jnp.sum(jnp.where(bias_mask, product, 0.0), axis=0, keepdims=True))
    bias_send[...] = jnp.concatenate(local_bias, axis=0).astype(BF16)

    for load in loads[5:]:
        load.wait()
    mask_row = big_negative * (mask[...].astype(F32) - 1.0)
    mask_column = jnp.broadcast_to(mask_row, (128, length)).T[:, :1]

    pl.semaphore_wait(barrier, n - 1)

    def scatter(step):
        peer = peer_of(step)
        pltpu.make_async_remote_copy(
            src_ref=send.at[peer], dst_ref=recv.at[me],
            send_sem=send_sems.at[0], recv_sem=recv_sems.at[0],
            device_id=base + peer, device_id_type=LOGICAL,
        ).start()

    def spread_bias(step):
        peer = peer_of(step)
        pltpu.make_async_remote_copy(
            src_ref=bias_send, dst_ref=bias_recv.at[lax.rem(me, 2), me // 2],
            send_sem=send_sems.at[1], recv_sem=recv_sems.at[1],
            device_id=base + peer, device_id_type=LOGICAL,
        ).start()

    for step in range(n - 2, 0, -2):
        spread_bias(step)
    each_peer(n, scatter)
    recv[me] = send[me]
    bias_recv[lax.rem(me, 2), me // 2] = bias_send[...]

    def wait_all(ref, semaphore):
        whole = ref.at[pl.ds(0, n - 1)]
        pltpu.make_async_copy(whole, whole, semaphore).wait()

    mine, others = lax.rem(me, 2), 1 - lax.rem(me, 2)
    most = bias_recv.at[0, pl.ds(0, n // 2 - 1)]
    pltpu.make_async_copy(most, most, recv_sems.at[1]).wait()
    swap = pltpu.make_async_remote_copy(
        src_ref=bias_recv.at[mine], dst_ref=bias_recv.at[mine],
        send_sem=swap_sems.at[0], recv_sem=swap_sems.at[1],
        device_id=base + peer_of(1), device_id_type=LOGICAL,
    )
    swap.start()
    wait_all(recv, recv_sems.at[0])

    rows[...] = recv[...].astype(F32).reshape(n * local * local, channels)
    keys_count = n * local
    columns = [rows[pl.ds(column, keys_count, stride=local), :].astype(BF16) for column in range(local)]
    query_mask = head_mask(lanes, inner, window, size)
    key_value = dot(jnp.concatenate(columns, axis=0), proj[:, inner : 3 * inner]).astype(BF16)
    tops = jnp.concatenate([column[:window] for column in columns], axis=0)
    queries = dot(tops, proj[:, :inner]) * size ** (-0.5)
    gating = jax.nn.sigmoid(dot(tops, proj[:, 3 * inner :]) + gate[...])
    swap.wait()
    bias = jnp.stack([bias_recv[0], bias_recv[1]], axis=1).astype(F32).reshape(keys_count, lanes)
    attended = []
    for column in range(local):
        keys = key_value[column * keys_count : (column + 1) * keys_count, :inner]
        held = key_value[column * keys_count : (column + 1) * keys_count, inner:]
        query = queries[column * window : (column + 1) * window]
        query = jnp.where(query_mask, jnp.concatenate([query] * heads, axis=0), 0.0).astype(BF16)
        scores = dot(keys, query, 1, 1) + bias + mask_column
        weights = jnp.exp(scores - jnp.max(scores, axis=0, keepdims=True))
        totals = jnp.sum(weights, axis=0, keepdims=True)
        weights = (weights * (1.0 / totals)).astype(BF16)
        mixture = jnp.where(query_mask, dot(weights, held, 0, 0), 0.0)
        attended.append(jnp.sum(mixture.reshape(heads, window, inner), axis=0))
    gated = (gating * jnp.concatenate(attended, axis=0)).astype(BF16)
    update = dot(gated, wout[...]) + oshift[...]
    for column in range(local):
        mixed[pl.ds(column, window, stride=local), :] = update[column * window : (column + 1) * window]
    back[...] = mixed[...].reshape(n, WD * local, channels).astype(BF16)

    def give_back(step):
        peer = peer_of(step)
        pltpu.make_async_remote_copy(
            src_ref=back.at[peer], dst_ref=out_ref.at[me],
            send_sem=send_sems.at[2], recv_sem=recv_sems.at[2],
            device_id=base + peer, device_id_type=LOGICAL,
        ).start()

    each_peer(n, give_back)
    out_ref[me] = back[me]
    wait_all(out_ref, recv_sems.at[2])
    wait_all(recv, send_sems.at[0])
    pltpu.make_async_copy(most, most, send_sems.at[1]).wait()
    wait_all(out_ref, send_sems.at[2])


def per_device(
    pair_mantissa,
    pair_exponent,
    residue_mask,
    ln_gain,
    ln_shift,
    w_proj,
    w_bias,
    gate_shift,
    w_out,
    out_shift,
):
    n = lax.axis_size("row")
    local, length, channels = pair_mantissa.shape
    heads = w_bias.shape[1]
    lanes = heads * WD * n
    args = (
        pair_mantissa, pair_exponent, residue_mask[None], ln_gain[None], ln_shift[None],
        w_proj, w_bias.T, gate_shift[None], w_out, out_shift[None],
    )
    result = pl.pallas_call(
        functools.partial(kernel, n, heads),
        out_shape=pltpu.VMEM((n, WD * local, channels), BF16),
        in_specs=[pl.BlockSpec(memory_space=pl.ANY)] * len(args),
        out_specs=pl.BlockSpec(memory_space=pltpu.VMEM),
        scratch_shapes=[pltpu.VMEM(arg.shape, arg.dtype) for arg in args]
        + [
            pltpu.VMEM((n, local * local, channels), BF16),
            pltpu.VMEM((n, local * local, channels), BF16),
            pltpu.VMEM((local, lanes), BF16),
            pltpu.VMEM((2, n // 2, local, lanes), BF16),
            pltpu.VMEM((n * local * local, channels), F32),
            pltpu.VMEM((n * WD * local, channels), F32),
            pltpu.VMEM((n, WD * local, channels), BF16),
            pltpu.SemaphoreType.DMA((len(args),)),
            pltpu.SemaphoreType.DMA((3,)),
            pltpu.SemaphoreType.DMA((3,)),
            pltpu.SemaphoreType.DMA((2,)),
        ],
        compiler_params=pltpu.CompilerParams(collective_id=0, has_side_effects=True),
    )(*args)
    return result.reshape(WD, length, channels)


def solution(mesh):
    in_specs = (
        P(("groups", "row"), None, None),
        P(("groups", "row"), None, None),
        P("groups"),
        P(),
        P(),
        P(),
        P(),
        P(),
        P(),
        P(),
    )
    out_specs = P(("groups", "row"), None, None)
    return jax.shard_map(
        per_device, mesh=mesh, in_specs=in_specs, out_specs=out_specs, check_vma=False
    )
```

```python
import functools

import jax
import jax.numpy as jnp
from jax import lax
from jax.experimental import pallas as pl
from jax.experimental.pallas import tpu as pltpu
from jax.sharding import PartitionSpec as P

WD = 1

epsilon = 1e-05
big_negative = 1000000000.0
LOGICAL = pl.DeviceIdType.LOGICAL
F32 = jnp.float32
BF16 = jnp.bfloat16


def dot(a, b, ca=1, cb=0):
    return lax.dot_general(a, b, (((ca,), (cb,)), ((), ())), preferred_element_type=F32)


def head_mask(rows, lanes, row_group, lane_group):
    row_head = lax.broadcasted_iota(jnp.int32, (rows, lanes), 0) // row_group
    lane_head = lax.broadcasted_iota(jnp.int32, (rows, lanes), 1) // lane_group
    return row_head == lane_head


def each_peer(n, body):
    for step in range(n - 1, 0, -1):
        body(step)


def kernel(
    n, heads,
    mant_hbm, expo_hbm, mask_hbm, gain_hbm, shift_hbm, proj_hbm, wbias_hbm, gate_hbm, wout_hbm, oshift_hbm,
    out_ref,
    mant, expo, mask, gain, shift, proj, wbias, gate, wout, oshift,
    send, recv, bias_send, bias_recv, rows, mixed, back,
    load_sems, send_sems, recv_sems, swap_sems,
):
    me = lax.axis_index("row")
    base = lax.axis_index("groups") * n

    flips, rest = [], me
    while len(flips) < (n - 1).bit_length():
        flips.append((1 - 2 * lax.rem(rest, 2)) * 2 ** len(flips))
        rest = rest // 2

    def peer_of(step):
        return me + sum(flip for bit, flip in enumerate(flips) if step >> bit & 1)

    local, length, channels = mant.shape
    inner = wout.shape[0]
    window = WD * n
    size = inner // heads
    lanes = heads * window

    barrier = pltpu.get_barrier_semaphore()

    def greet(step):
        pl.semaphore_signal(barrier, inc=1, device_id=base + peer_of(step), device_id_type=LOGICAL)

    each_peer(n, greet)

    loads = [
        pltpu.make_async_copy(src, dst, load_sems.at[number])
        for number, (src, dst) in enumerate(
            [
                (mant_hbm, mant), (expo_hbm, expo), (gain_hbm, gain), (shift_hbm, shift), (wbias_hbm, wbias),
                (mask_hbm, mask), (proj_hbm, proj), (gate_hbm, gate), (wout_hbm, wout), (oshift_hbm, oshift),
            ]
        )
    ]
    for load in loads:
        load.start()

    for load in loads[:5]:
        load.wait()
    exponent = expo[...]
    scaling = jnp.zeros(exponent.shape, F32)
    for level in range(-3, 4):
        scaling = scaling + jnp.where(exponent == level, F32(2.0**level), F32(0.0))
    blocks = exponent.shape[1]
    values = mant[...].astype(F32).reshape(local, blocks, length // blocks, channels) * scaling[:, :, None, :]
    values = values.reshape(local * length, channels)
    center = jnp.mean(values, axis=-1, keepdims=True)
    values = values - center
    spread = jnp.mean(jnp.square(values), axis=-1, keepdims=True)
    normal = values * lax.rsqrt(spread + epsilon) * gain[...] + shift[...]

    split = normal.reshape(local, length // 8, 8, channels)
    low = lax.broadcasted_iota(jnp.int32, (length // 8, 8, channels), 1) < local
    even, odd = [], []
    for pair in range(0, local, 2):
        one, two = split[pair], split[pair + 1]
        even.append(jnp.where(low, one, pltpu.roll(two, local, 1)))
        odd.append(jnp.where(low, pltpu.roll(one, local, 1), two))
    pairs = jnp.stack([jnp.concatenate(even, axis=1), jnp.concatenate(odd, axis=1)], axis=1)
    send[...] = pairs.reshape(n, local * local, channels).astype(BF16)

    rounded = normal.astype(BF16).reshape(local, length, channels)
    bias_mask = head_mask(heads, lanes, 1, window)
    local_bias = []
    for row in range(local):
        repeated = jnp.concatenate([rounded[row, :window]] * heads, axis=0)
        product = dot(wbias[...], repeated, 1, 1)
        local_bias.append(jnp.sum(jnp.where(bias_mask, product, 0.0), axis=0, keepdims=True))
    bias_send[...] = jnp.concatenate(local_bias, axis=0).astype(BF16)

    for load in loads[5:]:
        load.wait()
    mask_row = big_negative * (mask[...].astype(F32) - 1.0)
    mask_column = jnp.broadcast_to(mask_row, (128, length)).T[:, :1]

    pl.semaphore_wait(barrier, n - 1)

    def scatter(step):
        peer = peer_of(step)
        pltpu.make_async_remote_copy(
            src_ref=send.at[peer], dst_ref=recv.at[me],
            send_sem=send_sems.at[0], recv_sem=recv_sems.at[0 if step < n // 2 else 3],
            device_id=base + peer, device_id_type=LOGICAL,
        ).start()

    def spread_bias(step):
        peer = peer_of(step)
        pltpu.make_async_remote_copy(
            src_ref=bias_send, dst_ref=bias_recv.at[lax.rem(me, 2), me // 2],
            send_sem=send_sems.at[1], recv_sem=recv_sems.at[1],
            device_id=base + peer, device_id_type=LOGICAL,
        ).start()

    for step in range(n - 2, 0, -2):
        spread_bias(step)
    each_peer(n, scatter)
    recv[me] = send[me]
    bias_recv[lax.rem(me, 2), me // 2] = bias_send[...]

    def wait_all(ref, semaphore):
        whole = ref.at[pl.ds(0, n - 1)]
        pltpu.make_async_copy(whole, whole, semaphore).wait()

    mine = lax.rem(me, 2)
    most = bias_recv.at[0, pl.ds(0, n // 2 - 1)]
    pltpu.make_async_copy(most, most, recv_sems.at[1]).wait()
    swap = pltpu.make_async_remote_copy(
        src_ref=bias_recv.at[mine], dst_ref=bias_recv.at[mine],
        send_sem=swap_sems.at[0], recv_sem=swap_sems.at[1],
        device_id=base + peer_of(1), device_id_type=LOGICAL,
    )
    swap.start()
    half, count = me // (n // 2), n // 2 * local * local
    for number, part in ((0, half), (3, 1 - half)):
        expected = recv.at[pl.ds(0, n // 2 - (number == 0))]
        pltpu.make_async_copy(expected, expected, recv_sems.at[number]).wait()
        arrived = recv[pl.ds(part * (n // 2), n // 2)]
        rows[pl.ds(pl.multiple_of(part * count, count), count), :] = arrived.astype(F32).reshape(count, channels)
    keys_count = n * local
    columns = [rows[pl.ds(column, keys_count, stride=local), :].astype(BF16) for column in range(local)]
    query_mask = head_mask(lanes, inner, window, size)
    key_value = dot(jnp.concatenate(columns, axis=0), proj[:, inner : 3 * inner]).astype(BF16)
    tops = jnp.concatenate([column[:window] for column in columns], axis=0)
    queries = dot(tops, proj[:, :inner]) * size ** (-0.5)
    gating = jax.nn.sigmoid(dot(tops, proj[:, 3 * inner :]) + gate[...])
    swap.wait()
    bias = jnp.stack([bias_recv[0], bias_recv[1]], axis=1).astype(F32).reshape(keys_count, lanes)
    attended = []
    for column in range(local):
        keys = key_value[column * keys_count : (column + 1) * keys_count, :inner]
        held = key_value[column * keys_count : (column + 1) * keys_count, inner:]
        query = queries[column * window : (column + 1) * window]
        query = jnp.where(query_mask, jnp.concatenate([query] * heads, axis=0), 0.0).astype(BF16)
        scores = dot(keys, query, 1, 1) + bias + mask_column
        weights = jnp.exp(scores - jnp.max(scores, axis=0, keepdims=True))
        totals = jnp.sum(weights, axis=0, keepdims=True)
        weights = (weights * (1.0 / totals)).astype(BF16)
        mixture = jnp.where(query_mask, dot(weights, held, 0, 0), 0.0)
        attended.append(jnp.sum(mixture.reshape(heads, window, inner), axis=0))
    gated = (gating * jnp.concatenate(attended, axis=0)).astype(BF16)
    update = dot(gated, wout[...]) + oshift[...]
    for column in range(local):
        mixed[pl.ds(column, window, stride=local), :] = update[column * window : (column + 1) * window]
    back[...] = mixed[...].reshape(n, WD * local, channels).astype(BF16)

    def give_back(step):
        peer = peer_of(step)
        pltpu.make_async_remote_copy(
            src_ref=back.at[peer], dst_ref=out_ref.at[me],
            send_sem=send_sems.at[2], recv_sem=recv_sems.at[2],
            device_id=base + peer, device_id_type=LOGICAL,
        ).start()

    each_peer(n, give_back)
    out_ref[me] = back[me]
    wait_all(recv, send_sems.at[0])
    pltpu.make_async_copy(most, most, send_sems.at[1]).wait()
    wait_all(out_ref, send_sems.at[2])
    wait_all(out_ref, recv_sems.at[2])


def per_device(
    pair_mantissa,
    pair_exponent,
    residue_mask,
    ln_gain,
    ln_shift,
    w_proj,
    w_bias,
    gate_shift,
    w_out,
    out_shift,
):
    n = lax.axis_size("row")
    local, length, channels = pair_mantissa.shape
    heads = w_bias.shape[1]
    lanes = heads * WD * n
    args = (
        pair_mantissa, pair_exponent, residue_mask[None], ln_gain[None], ln_shift[None],
        w_proj, w_bias.T, gate_shift[None], w_out, out_shift[None],
    )
    result = pl.pallas_call(
        functools.partial(kernel, n, heads),
        out_shape=pltpu.VMEM((n, WD * local, channels), BF16),
        in_specs=[pl.BlockSpec(memory_space=pl.ANY)] * len(args),
        out_specs=pl.BlockSpec(memory_space=pltpu.VMEM),
        scratch_shapes=[pltpu.VMEM(arg.shape, arg.dtype) for arg in args]
        + [
            pltpu.VMEM((n, local * local, channels), BF16),
            pltpu.VMEM((n, local * local, channels), BF16),
            pltpu.VMEM((local, lanes), BF16),
            pltpu.VMEM((2, n // 2, local, lanes), BF16),
            pltpu.VMEM((n * local * local, channels), F32),
            pltpu.VMEM((n * WD * local, channels), F32),
            pltpu.VMEM((n, WD * local, channels), BF16),
            pltpu.SemaphoreType.DMA((len(args),)),
            pltpu.SemaphoreType.DMA((3,)),
            pltpu.SemaphoreType.DMA((4,)),
            pltpu.SemaphoreType.DMA((2,)),
        ],
        compiler_params=pltpu.CompilerParams(collective_id=0, has_side_effects=True),
    )(*args)
    return result.reshape(WD, length, channels)


def solution(mesh):
    in_specs = (
        P(("groups", "row"), None, None),
        P(("groups", "row"), None, None),
        P("groups"),
        P(),
        P(),
        P(),
        P(),
        P(),
        P(),
        P(),
    )
    out_specs = P(("groups", "row"), None, None)
    return jax.shard_map(
        per_device, mesh=mesh, in_specs=in_specs, out_specs=out_specs, check_vma=False
    )
```
